32 devices in a mesh: groups: 2 (over y), row: 8 (over z, x), rep: 2 (over core).
Axes of the slice: x: 2, y: 2, z: 4, core: 2. Of those that a mesh axis runs over, the one named last changes fastest.
Arguments:
- features: bfloat16 [4096, 128], P(('groups', 'row', 'rep')), parts along dimension 0, may hold values from -6 to 6
- adjacency: bfloat16 [4096, 128, 128], P(('groups', 'row', 'rep')), parts along dimension 0, may hold values from -0.078125 to 0.078125
- tile_row: int32 [4096], P(('groups', 'row', 'rep')), parts along dimension 0, may hold values from 0 to 1
- tile_col: int32 [4096], P(('groups', 'row', 'rep')), parts along dimension 0, may hold values from 0 to 7
- tile_count: int32 [32], P(('groups', 'row', 'rep')), parts along dimension 0, may hold values from 64 to 128, as said below
- weight_in: bfloat16 [128, 512], replicated, may hold values from -0.5 to 0.5
- weight_out: bfloat16 [512, 48], replicated, may hold values from -0.25 to 0.25
- cotangent: bfloat16 [4096, 48], P(('groups', 'row', 'rep')), parts along dimension 0
Outputs:
- logits: float32 [4096, 48], P(('groups', 'row', 'rep')), parts along dimension 0
- grad_in: float32 [256, 512], P('groups'), parts along dimension 0
- grad_out: float32 [1024, 48], P('groups'), parts along dimension 0
The draws below stay inside these ranges and needn't reach their ends.
There are 2 independent parts, one for each index of `groups`. The reference program is written for one: setup_inputs(seed, part) draws one part's arguments, and reference() takes and returns one part's arrays. A program takes and returns all parts, laid end to end along the dimension named above; an argument that names none is the same for every part. Nothing has to cross between parts.
Inputs may be any that keep to these rules, and one draw needn't show every extreme that they name: `tile_count`: each shard uses at least half of its slots, and some shard uses all 128.
All inputs are finite; a program needn't handle non-finite values.
Results may differ from the reference program's by a relative error of at most 0.015.
Values may be sent and summed in bfloat16 or wider, within the bound.
No kernel may reach another device: no remote copies, remote signals or barrier semaphores. Data moves between devices by JAX's collectives and lax.ppermute only.
A program may use at most 64 MiB of HBM per device.

```python
import jax
import jax.numpy as jnp
from jax import lax

TILE = 128
IN = 128
DH = 512
C = 48
TILES = 128
BLOCKS = 8
REPLICAS = 2
SHARDS = 16
NODES = 2048


def draw_tile_count(key, part):
    first, second = jax.random.split(jax.random.fold_in(key, 11))
    counts = jax.random.randint(first, (SHARDS,), max(1, TILES // 2), TILES + 1)
    where = jax.random.randint(second, (), 0, SHARDS)
    return counts.at[where].set(TILES).astype(jnp.int32)


def draw_cotangent(key, part):
    first = jax.random.fold_in(jax.random.fold_in(key, 23), 0)
    position = jnp.arange(NODES, dtype=jnp.float32)[:, None] / NODES
    rise = jnp.exp(jnp.log(3.0) * position)
    base = jax.random.normal(first, (NODES, C), jnp.float32)
    return (base * rise * (2.0 / NODES ** 0.5)).astype(jnp.bfloat16)


def plant(result, rng, smallest, top_value):
    extent = result.shape
    spot = [jax.random.randint(jax.random.fold_in(rng, axis), (), 0, extent[axis]) for axis in range(len(extent))]
    result = result.at[tuple(spot)].set(smallest)
    longest = extent.index(max(extent))
    spot[longest] = (spot[longest] + 1) % extent[longest]
    return result.at[tuple(spot)].set(top_value)


def shard_levels(stream_key, shape, shards, smallest, top_value):
    factor_of, own = 1.0, jax.random.fold_in(stream_key, 6)
    for axis_at, shards_of in shards:
        draws = jnp.exp(jax.random.uniform(jax.random.fold_in(own, axis_at), (shards_of,), jnp.float32, smallest / len(shards), top_value / len(shards)))
        factor_of = factor_of * jnp.repeat(draws, shape[axis_at] // shards_of).reshape([-1 if axis == axis_at else 1 for axis in range(len(shape))])
    return factor_of


def centred(rng, shape, scale, most, cuts=(), held_as=jnp.bfloat16):
    drawn = scale * jax.random.normal(rng, shape, jnp.float32)
    if cuts:
        drawn = drawn * shard_levels(rng, shape, cuts, -0.22, 0.18)
    return jnp.clip(drawn, -most, most).astype(held_as)


def setup_inputs(seed: int = 0, part: int = 0) -> dict:
    streams_of = jax.random.split(jax.random.key(seed), 9)
    own_keys = jax.random.split(jax.random.fold_in(streams_of[8], part), 9)
    features = centred(own_keys[0], (NODES, IN), 1.0, 6.0, ((0, 16),))
    adjacency = centred(own_keys[1], (SHARDS * TILES, TILE, TILE), (3 * TILES * TILE // 8) ** -0.5, 0.078125, ((0, 16),))
    tile_row = plant(jax.random.randint(own_keys[2], (SHARDS * TILES,), 0, REPLICAS), jax.random.fold_in(own_keys[2], 1), 0, REPLICAS - 1).astype(jnp.int32)
    tile_col = plant(jax.random.randint(own_keys[3], (SHARDS * TILES,), 0, BLOCKS), jax.random.fold_in(own_keys[3], 1), 0, BLOCKS - 1).astype(jnp.int32)
    tile_count = draw_tile_count(jax.random.fold_in(jax.random.fold_in(streams_of[8], part), 71), part)
    weight_in = centred(streams_of[5], (IN, DH), IN ** -0.5, 0.5)
    weight_out = centred(streams_of[6], (DH, C), DH ** -0.5, 0.25)
    cotangent = draw_cotangent(jax.random.fold_in(jax.random.fold_in(streams_of[8], part), 71), part)
    return {"features": features, "adjacency": adjacency, "tile_row": tile_row, "tile_col": tile_col, "tile_count": tile_count, "weight_in": weight_in, "weight_out": weight_out, "cotangent": cotangent}


def expand(adjacency, tile_row, tile_col, tile_count):
    tile_vals = adjacency.reshape(SHARDS, TILES, TILE, TILE).astype(jnp.float32)
    usable = (jnp.arange(TILES)[None, :] < tile_count[:, None]).astype(jnp.float32)
    row_ids = tile_row.reshape(SHARDS, TILES)
    row_hot = (row_ids[:, None, :] == jnp.arange(REPLICAS)[None, :, None]).astype(jnp.float32) * usable[:, None, :]
    return tile_vals, row_hot, tile_col.reshape(SHARDS, TILES)


def aggregate(source, tile_vals, row_hot, columns):
    width = source.shape[1]
    pieces = source.astype(jnp.float32).reshape(BLOCKS, REPLICAS, TILE, width)

    def one_shard(index):
        part_of = index % REPLICAS
        picked = pieces[:, part_of][columns[index]]
        products = jnp.einsum('tab,tbw->taw', tile_vals[index], picked)
        return jnp.einsum('pt,taw->paw', row_hot[index], products)

    partial_value = lax.map(one_shard, jnp.arange(SHARDS))
    summed = partial_value.reshape(BLOCKS, REPLICAS, REPLICAS, TILE, width).sum(axis=1)
    return summed.reshape(NODES, width)


def transpose(source, tile_vals, row_hot, columns):
    width = source.shape[1]
    block_vals = source.astype(jnp.float32).reshape(BLOCKS, REPLICAS, TILE, width)

    def one_shard(total, index):
        block = index // REPLICAS
        part_of = index % REPLICAS
        picked = jnp.einsum('pt,paw->taw', row_hot[index], block_vals[block])
        contrib = jnp.einsum('tab,taw->tbw', tile_vals[index], picked)
        col_hot = (columns[index][None, :] == jnp.arange(BLOCKS)[:, None]).astype(block_vals.dtype)
        placed = jnp.einsum('jt,tbw->jbw', col_hot, contrib)
        return total.at[:, part_of].add(placed), None

    start = jnp.zeros((BLOCKS, REPLICAS, TILE, width), block_vals.dtype)
    total, _ = lax.scan(one_shard, start, jnp.arange(SHARDS))
    return total.reshape(NODES, width)


def reference(features, adjacency, tile_row, tile_col, tile_count, weight_in, weight_out, cotangent):
    tile_vals, row_hot, columns = expand(adjacency, tile_row, tile_col, tile_count)
    aggregated = aggregate(features, tile_vals, row_hot, columns).astype(jnp.bfloat16)
    pre_act = jnp.dot(aggregated, weight_in, preferred_element_type=jnp.float32)
    hidden = jax.nn.silu(pre_act).astype(jnp.bfloat16)
    projected = jnp.dot(hidden, weight_out, preferred_element_type=jnp.float32).astype(jnp.bfloat16)
    logits = aggregate(projected, tile_vals, row_hot, columns)
    back_round = transpose(cotangent, tile_vals, row_hot, columns).astype(jnp.bfloat16)
    grad_out = jnp.dot(hidden.T, back_round, preferred_element_type=jnp.float32)
    sigmoid_of = jax.nn.sigmoid(pre_act)
    back_hidden = jnp.dot(back_round, weight_out.T, preferred_element_type=jnp.float32)
    grad_pre = (back_hidden * sigmoid_of * (1.0 + pre_act * (1.0 - sigmoid_of))).astype(jnp.bfloat16)
    grad_in = jnp.dot(aggregated.T, grad_pre, preferred_element_type=jnp.float32)
    return logits, grad_in, grad_out
```

```python
import functools

import jax
import jax.numpy as jnp
from jax import lax
from jax.experimental import pallas as pl
from jax.experimental.pallas import tpu as pltpu
from jax.sharding import PartitionSpec as P

F32 = jnp.float32
BF16 = jnp.bfloat16
VMEM = pl.BlockSpec(memory_space=pltpu.VMEM)
SMEM = pl.BlockSpec(memory_space=pltpu.SMEM)
ANY = pl.BlockSpec(memory_space=pl.ANY)
MIB = 1 << 20


def dot(a, b, ca=1, cb=0):
    return lax.dot_general(a, b, (((ca,), (cb,)), ((), ())), preferred_element_type=F32)


def densify_kernel(
    blocks, chunks, row_ref, col_ref, count_ref, adj_ref, own_ref, other_ref, a_ref, term_ref, tiles, total, sems
):
    slots, edge = tiles.shape[0], tiles.shape[1]
    per = slots // chunks
    rep = lax.axis_index("rep")
    count = count_ref[0]

    def copy(k):
        part = pl.ds(k * per, per)
        return pltpu.make_async_copy(adj_ref.at[part], tiles.at[part], sems.at[k])

    for k in range(chunks):
        copy(k).start()

    @pl.loop(0, 2 * blocks)
    def _(i):
        total[i] = jnp.zeros((edge, edge), F32)

    for k in range(chunks):
        copy(k).wait()

        @pl.loop(k * per, (k + 1) * per, unroll=4)
        def _(t):
            where = jnp.bitwise_xor(row_ref[t], rep) * blocks + col_ref[t]
            where = jnp.where(t < count, where, 2 * blocks)
            total[where] += tiles[t].astype(F32)

    own, other = own_ref[...], other_ref[...]

    @pl.loop(0, blocks, unroll=min(blocks, 8))
    def _(j):
        at = pl.ds(pl.multiple_of(j * edge, edge), edge)
        first = total[j].astype(BF16)
        second = total[blocks + j].astype(BF16)
        a_ref[0, :, at] = first
        a_ref[1, :, at] = second
        term_ref[j] = dot(own, first) + dot(other, second)


def densify(tile_row, tile_col, tile_count, adjacency, own, other, blocks):
    slots, edge, _ = adjacency.shape
    chunks = 8
    return pl.pallas_call(
        functools.partial(densify_kernel, blocks, chunks),
        out_shape=(
            jax.ShapeDtypeStruct((2, edge, blocks * edge), BF16),
            jax.ShapeDtypeStruct((blocks, own.shape[0], edge), F32),
        ),
        in_specs=[SMEM, SMEM, SMEM, ANY, VMEM, VMEM],
        out_specs=(VMEM, VMEM),
        scratch_shapes=[
            pltpu.VMEM((slots, edge, edge), BF16),
            pltpu.VMEM((2 * blocks + 1, edge, edge), F32),
            pltpu.SemaphoreType.DMA((chunks,)),
        ],
        compiler_params=pltpu.CompilerParams(vmem_limit_bytes=48 * MIB),
        cost_estimate=pl.CostEstimate(flops=10**9, bytes_accessed=12 * 10**6, transcendentals=0),
        name="densify",
    )(tile_row, tile_col, tile_count, adjacency, own, other)


def aggregate_kernel(a_ref, x_ref, own_ref, other_ref):
    x = x_ref[...]
    own_ref[...] = dot(a_ref[0], x)
    other_ref[...] = dot(a_ref[1], x)


def aggregate(a, x):
    edge, width = a.shape[1], x.shape[1]
    part = jax.ShapeDtypeStruct((edge, width), F32)
    return pl.pallas_call(
        aggregate_kernel,
        out_shape=(part, part),
        in_specs=[VMEM, VMEM],
        out_specs=(VMEM, VMEM),
        compiler_params=pltpu.CompilerParams(vmem_limit_bytes=40 * MIB),
        cost_estimate=pl.CostEstimate(flops=10**8, bytes_accessed=10**6, transcendentals=0),
        name="aggregate",
    )(a, x)


def spread_kernel(a_ref, b_ref, o_ref):
    value = (a_ref[...] + b_ref[...]).astype(BF16)

    @pl.loop(0, o_ref.shape[0])
    def _(j):
        o_ref[j] = value


def spread_sum_kernel(x_ref, o_ref):
    blocks = x_ref.shape[0]
    total = x_ref[0]
    total = lax.fori_loop(1, blocks, lambda j, t: t + x_ref[j], total)
    value = total.astype(BF16)

    @pl.loop(0, blocks)
    def _(j):
        o_ref[j] = value


def small_call(kernel, shape, name, *args):
    return pl.pallas_call(
        kernel,
        out_shape=jax.ShapeDtypeStruct(shape, BF16),
        in_specs=[VMEM] * len(args),
        out_specs=VMEM,
        compiler_params=pltpu.CompilerParams(vmem_limit_bytes=32 * MIB),
        cost_estimate=pl.CostEstimate(flops=10**5, bytes_accessed=5 * 10**5, transcendentals=0),
        name=name,
    )(*args)


def logits_kernel(agg_ref, win_ref, wout_ref, a_ref, own_ref, other_ref, own_acc, other_acc):
    step = pl.program_id(0)

    @pl.when(step == 0)
    def _():
        own_acc[...] = jnp.zeros_like(own_acc)
        other_acc[...] = jnp.zeros_like(other_acc)

    pre = dot(agg_ref[...], win_ref[...])
    hidden = jax.nn.silu(pre).astype(BF16)
    projected = dot(wout_ref[...], hidden, 1, 1).astype(BF16)
    own_acc[...] += dot(projected, a_ref[0], 1, 1)
    other_acc[...] += dot(projected, a_ref[1], 1, 1)

    @pl.when(step == pl.num_programs(0) - 1)
    def _():
        own_ref[...] = own_acc[...]
        other_ref[...] = other_acc[...]


def logits_parts(agg, win, wout, a):
    nodes, width = agg.shape
    classes, edge = wout.shape[0], a.shape[1]
    hidden = win.shape[1]
    step = min(nodes, 1024)
    part = jax.ShapeDtypeStruct((classes, edge), F32)
    keep = pl.BlockSpec((classes, edge), lambda i: (0, 0))
    return pl.pallas_call(
        logits_kernel,
        grid=(nodes // step,),
        out_shape=(part, part),
        in_specs=[
            pl.BlockSpec((step, width), lambda i: (i, 0)),
            pl.BlockSpec((width, hidden), lambda i: (0, 0)),
            pl.BlockSpec((classes, hidden), lambda i: (0, 0)),
            pl.BlockSpec((2, edge, step), lambda i: (0, 0, i)),
        ],
        out_specs=(keep, keep),
        scratch_shapes=[pltpu.VMEM((classes, edge), F32)] * 2,
        compiler_params=pltpu.CompilerParams(vmem_limit_bytes=32 * MIB),
        cost_estimate=pl.CostEstimate(flops=4 * 10**8, bytes_accessed=10**6, transcendentals=10**6),
        name="logits",
    )(agg, win, wout, a)


def grads_kernel(agg_ref, back_ref, win_ref, wout_ref, gin_ref, gout_ref):
    step = pl.program_id(1)
    agg = agg_ref[...].reshape(-1, agg_ref.shape[-1])
    pre = dot(agg, win_ref[...])
    sig = jax.nn.sigmoid(pre)
    hidden = (pre * sig).astype(BF16)
    gate = sig * (1.0 + pre * (1.0 - sig))
    back = back_ref[...]
    many, classes, edge = back.shape
    back = jnp.concatenate([back[j] for j in range(many)], axis=1)
    grad_pre = (dot(back, wout_ref[...], 0, 0) * gate).astype(BF16)
    gin = dot(agg, grad_pre, 0, 0)
    gout = dot(back, hidden)

    @pl.when(step == 0)
    def _():
        gin_ref[...] = gin
        gout_ref[...] = gout

    @pl.when(step > 0)
    def _():
        gin_ref[...] += gin
        gout_ref[...] += gout


def grads(agg, back, win, wout):
    blocks, edge, width = agg.shape
    classes, hidden = wout.shape
    step = min(blocks, 8)
    return pl.pallas_call(
        grads_kernel,
        grid=(1, blocks // step),
        out_shape=(
            jax.ShapeDtypeStruct((width, hidden), F32),
            jax.ShapeDtypeStruct((classes, hidden), F32),
        ),
        in_specs=[
            pl.BlockSpec((step, edge, width), lambda h, i: (i, 0, 0)),
            pl.BlockSpec((step, classes, edge), lambda h, i: (i, 0, 0)),
            pl.BlockSpec((width, hidden), lambda h, i: (0, 0)),
            pl.BlockSpec((classes, hidden), lambda h, i: (0, 0)),
        ],
        out_specs=(
            pl.BlockSpec((width, hidden), lambda h, i: (0, 0)),
            pl.BlockSpec((classes, hidden), lambda h, i: (0, 0)),
        ),
        compiler_params=pltpu.CompilerParams(vmem_limit_bytes=48 * MIB),
        cost_estimate=pl.CostEstimate(flops=6 * 10**8, bytes_accessed=10**6, transcendentals=10**6),
        name="grads",
    )(agg, back, win, wout)


def shards(features, adjacency, tile_row, tile_col, tile_count, weight_in, weight_out, cotangent):
    blocks = lax.axis_size("row")
    edge = adjacency.shape[1]
    width = features.shape[1]
    classes = weight_out.shape[1]

    def exchange(x):
        return lax.all_to_all(x, "row", split_axis=0, concat_axis=0, tiled=True)

    def swap(x):
        return lax.ppermute(x, "rep", [(0, 1), (1, 0)])

    wout = weight_out.T
    cot = cotangent.T
    gathered = exchange(jnp.broadcast_to(features[None], (blocks, edge, width)))
    a, terms = densify(tile_row, tile_col, tile_count, adjacency, cot, swap(cot), blocks)
    arrived = exchange(terms)
    own, other = aggregate(a, gathered.reshape(blocks * edge, width))
    agg_all = exchange(small_call(spread_kernel, (blocks, edge, width), "spread_agg", own, swap(other)))
    back_all = exchange(small_call(spread_sum_kernel, (blocks, classes, edge), "spread_back", arrived))
    logit_own, logit_other = logits_parts(agg_all.reshape(blocks * edge, width), weight_in, wout, a)
    logits = logit_own + swap(logit_other)
    gin, gout = grads(agg_all, back_all, weight_in, wout)
    grad_in = gin + swap(gin)
    grad_out = gout + swap(gout)
    return (logits.T, grad_in, grad_out.T)


def solution(mesh):
    in_specs = (
        P(("groups", "row", "rep"), None),
        P(("groups", "row", "rep"), None, None),
        P(("groups", "row", "rep")),
        P(("groups", "row", "rep")),
        P(("groups", "row", "rep")),
        P(),
        P(),
        P(("groups", "row", "rep"), None),
    )
    out_specs = (P(("groups", "row", "rep"), None), P("groups", None), P("groups", None))
    return jax.shard_map(shards, mesh=mesh, in_specs=in_specs, out_specs=out_specs, check_vma=False)
```

```python
import functools

import jax
import jax.numpy as jnp
from jax import lax
from jax.experimental import pallas as pl
from jax.experimental.pallas import tpu as pltpu
from jax.sharding import PartitionSpec as P

F32 = jnp.float32
BF16 = jnp.bfloat16
VMEM = pl.BlockSpec(memory_space=pltpu.VMEM)
SMEM = pl.BlockSpec(memory_space=pltpu.SMEM)
HBM = pl.BlockSpec(memory_space=pltpu.HBM)
MIB = 1 << 20


def dot(a, b, ca=1, cb=0):
    return lax.dot_general(a, b, (((ca,), (cb,)), ((), ())), preferred_element_type=F32)


def densify_kernel(blocks, chunks, count_ref, row_hbm, col_hbm, adj_ref, a_ref, tiles, total, rows, cols, sems, small):
    slots, edge = tiles.shape[0], tiles.shape[1]
    per = slots // chunks
    rep = lax.axis_index("rep")

    def copy(k):
        part = pl.ds(k * per, per)
        return pltpu.make_async_copy(adj_ref.at[part], tiles.at[part], sems.at[k])

    tables = [
        pltpu.make_async_copy(src, dst, small.at[i])
        for i, (src, dst) in enumerate(((row_hbm, rows), (col_hbm, cols)))
    ]
    for table in tables:
        table.start()
    for k in range(chunks):
        copy(k).start()

    @pl.loop(0, 2 * blocks)
    def _(i):
        total[i] = jnp.zeros((edge, edge), F32)

    for table in tables:
        table.wait()
    count = count_ref[0]
    for k in range(chunks):
        copy(k).wait()

        @pl.loop(k * per, (k + 1) * per, unroll=4)
        def _(t):
            where = jnp.bitwise_xor(rows[t], rep) * blocks + cols[t]
            where = jnp.where(t < count, where, 2 * blocks)
            total[where] += tiles[t].astype(F32)

    @pl.loop(0, blocks, unroll=min(blocks, 8))
    def _(j):
        at = pl.ds(pl.multiple_of(j * edge, edge), edge)
        a_ref[0, :, at] = total[j].astype(BF16)
        a_ref[1, :, at] = total[blocks + j].astype(BF16)


def densify(tile_row, tile_col, tile_count, adjacency, blocks):
    slots, edge, _ = adjacency.shape
    chunks = 8
    return pl.pallas_call(
        functools.partial(densify_kernel, blocks, chunks),
        out_shape=jax.ShapeDtypeStruct((2, edge, blocks * edge), BF16),
        in_specs=[SMEM, HBM, HBM, HBM],
        out_specs=VMEM,
        scratch_shapes=[
            pltpu.VMEM((slots, edge, edge), BF16),
            pltpu.VMEM((2 * blocks + 1, edge, edge), F32),
            pltpu.SMEM((slots,), jnp.int32),
            pltpu.SMEM((slots,), jnp.int32),
            pltpu.SemaphoreType.DMA((chunks,)),
            pltpu.SemaphoreType.DMA((2,)),
        ],
        compiler_params=pltpu.CompilerParams(vmem_limit_bytes=48 * MIB),
        cost_estimate=pl.CostEstimate(flops=10**9, bytes_accessed=12 * 10**6, transcendentals=0),
        name="densify",
    )(tile_count, *(pltpu.with_memory_space_constraint(x, pltpu.HBM) for x in (tile_row, tile_col, adjacency)))


def terms_kernel(a_ref, own_ref, other_ref, x_ref, o_ref):
    blocks, _, edge = o_ref.shape
    nodes = x_ref.shape[0]
    own, other, x = own_ref[...], other_ref[...], x_ref[...]

    @pl.loop(0, blocks, unroll=min(blocks, 8))
    def _(j):
        at = pl.ds(pl.multiple_of(j * edge, edge), edge)
        o_ref[j, :nodes, :] = x
        o_ref[j, nodes:, :] = (dot(own, a_ref[0, :, at]) + dot(other, a_ref[1, :, at])).astype(BF16)


def aggregate_kernel(a_ref, x_ref, own_ref, other_ref):
    blocks, _, width = x_ref.shape
    nodes = a_ref.shape[1]
    x = x_ref[:, :nodes, :].reshape(blocks * nodes, width)
    own_ref[...] = dot(a_ref[0], x)
    other_ref[...] = dot(a_ref[1], x)


def spread_kernel(a_ref, b_ref, x_ref, o_ref):
    blocks = x_ref.shape[0]
    nodes = a_ref.shape[0]
    total = x_ref[0, nodes:, :].astype(F32)
    total = lax.fori_loop(1, blocks, lambda j, t: t + x_ref[j, nodes:, :].astype(F32), total, unroll=min(blocks - 1, 7))
    value = jnp.concatenate([(a_ref[...] + b_ref[...]).astype(BF16), total.astype(BF16)], axis=0)

    @pl.loop(0, blocks, unroll=min(blocks, 8))
    def _(j):
        o_ref[j] = value


def small_call(kernel, out, name, flops, *args):
    return pl.pallas_call(
        kernel,
        out_shape=out,
        in_specs=[VMEM] * len(args),
        out_specs=jax.tree.map(lambda _: VMEM, out),
        compiler_params=pltpu.CompilerParams(vmem_limit_bytes=40 * MIB),
        cost_estimate=pl.CostEstimate(flops=flops, bytes_accessed=10**6, transcendentals=0),
        name=name,
    )(*args)


def logits_kernel(x_ref, win_ref, wout_ref, a_ref, own_ref, other_ref, own_acc, other_acc):
    step = pl.program_id(0)

    @pl.when(step == 0)
    def _():
        own_acc[...] = jnp.zeros_like(own_acc)
        other_acc[...] = jnp.zeros_like(other_acc)

    nodes = a_ref.shape[1]
    agg = x_ref[:, :nodes, :].reshape(-1, x_ref.shape[2])
    pre = dot(agg, win_ref[...])
    hidden = jax.nn.silu(pre).astype(BF16)
    projected = dot(wout_ref[...], hidden, 1, 1).astype(BF16)
    own_acc[...] += dot(projected, a_ref[0], 1, 1)
    other_acc[...] += dot(projected, a_ref[1], 1, 1)

    @pl.when(step == pl.num_programs(0) - 1)
    def _():
        own_ref[...] = own_acc[...]
        other_ref[...] = other_acc[...]


def logits_parts(x, win, wout, a):
    blocks, rows, width = x.shape
    classes, edge = wout.shape[0], a.shape[1]
    hidden = win.shape[1]
    step = min(blocks, 8)
    part = jax.ShapeDtypeStruct((classes, edge), F32)
    keep = pl.BlockSpec((classes, edge), lambda i: (0, 0))
    return pl.pallas_call(
        logits_kernel,
        grid=(blocks // step,),
        out_shape=(part, part),
        in_specs=[
            pl.BlockSpec((step, rows, width), lambda i: (i, 0, 0)),
            pl.BlockSpec((width, hidden), lambda i: (0, 0)),
            pl.BlockSpec((classes, hidden), lambda i: (0, 0)),
            pl.BlockSpec((2, edge, step * edge), lambda i: (0, 0, i)),
        ],
        out_specs=(keep, keep),
        scratch_shapes=[pltpu.VMEM((classes, edge), F32)] * 2,
        compiler_params=pltpu.CompilerParams(vmem_limit_bytes=32 * MIB),
        cost_estimate=pl.CostEstimate(flops=4 * 10**8, bytes_accessed=10**6, transcendentals=10**6),
        name="logits",
    )(x, win, wout, a)


def grads_kernel(x_ref, win_ref, wout_ref, o_ref):
    step = pl.program_id(0)
    many, rows, width = x_ref.shape
    classes = wout_ref.shape[0]
    nodes = rows - classes
    agg = x_ref[:, :nodes, :].reshape(-1, width)
    pre = dot(agg, win_ref[...])
    sig = jax.nn.sigmoid(pre)
    hidden = (pre * sig).astype(BF16)
    gate = sig * (1.0 + pre * (1.0 - sig))
    back = jnp.concatenate([x_ref[j, nodes:, :] for j in range(many)], axis=1)
    grad_pre = (dot(back, wout_ref[...], 0, 0) * gate).astype(BF16)
    gin = dot(agg, grad_pre, 0, 0)
    gout = dot(back, hidden)

    @pl.when(step == 0)
    def _():
        o_ref[:width, :] = gin
        o_ref[width:, :] = gout

    @pl.when(step > 0)
    def _():
        o_ref[:width, :] += gin
        o_ref[width:, :] += gout


def grads(x, win, wout):
    blocks, rows, width = x.shape
    classes, hidden = wout.shape
    step = min(blocks, 8)
    return pl.pallas_call(
        grads_kernel,
        grid=(blocks // step,),
        out_shape=jax.ShapeDtypeStruct((width + classes, hidden), F32),
        in_specs=[
            pl.BlockSpec((step, rows, width), lambda i: (i, 0, 0)),
            pl.BlockSpec((width, hidden), lambda i: (0, 0)),
            pl.BlockSpec((classes, hidden), lambda i: (0, 0)),
        ],
        out_specs=pl.BlockSpec((width + classes, hidden), lambda i: (0, 0)),
        compiler_params=pltpu.CompilerParams(vmem_limit_bytes=48 * MIB),
        cost_estimate=pl.CostEstimate(flops=6 * 10**8, bytes_accessed=10**6, transcendentals=10**6),
        name="grads",
    )(x, win, wout)


def finish_kernel(lo_ref, lr_ref, go_ref, gr_ref, logits_ref, gin_ref, gout_ref):
    width = gin_ref.shape[0]
    logits_ref[...] = lo_ref[...] + lr_ref[...]
    gin_ref[...] = go_ref[:width, :] + gr_ref[:width, :]
    gout_ref[...] = go_ref[width:, :] + gr_ref[width:, :]


def shards(features, adjacency, tile_row, tile_col, tile_count, weight_in, weight_out, cotangent):
    blocks = lax.axis_size("row")
    edge = adjacency.shape[1]
    width = features.shape[1]
    classes = weight_out.shape[1]

    def exchange(x):
        return lax.all_to_all(x, "row", split_axis=0, concat_axis=0, tiled=True)

    def swap(x):
        return lax.ppermute(x, "rep", [(0, 1), (1, 0)])

    wout = weight_out.T
    cot = cotangent.T
    hidden = weight_in.shape[1]

    def like(*shape, dtype=F32):
        return jax.ShapeDtypeStruct(shape, dtype)

    packed = like(blocks, edge + classes, width, dtype=BF16)
    a = densify(tile_row, tile_col, tile_count, adjacency, blocks)
    arrived = exchange(small_call(terms_kernel, packed, "terms", 10**8, a, cot, swap(cot), features))
    own, other = small_call(aggregate_kernel, (like(edge, width),) * 2, "aggregate", 10**8, a, arrived)
    held = exchange(small_call(spread_kernel, packed, "spread", 10**6, own, swap(other), arrived))
    logit_own, logit_other = logits_parts(held, weight_in, wout, a)
    grad = grads(held, weight_in, wout)
    logits, grad_in, grad_out = small_call(
        finish_kernel,
        (like(classes, edge), like(width, hidden), like(classes, hidden)),
        "finish",
        10**6,
        logit_own,
        swap(logit_other),
        grad,
        swap(grad),
    )
    return (logits.T, grad_in, grad_out.T)


def solution(mesh):
    in_specs = (
        P(("groups", "row", "rep"), None),
        P(("groups", "row", "rep"), None, None),
        P(("groups", "row", "rep")),
        P(("groups", "row", "rep")),
        P(("groups", "row", "rep")),
        P(),
        P(),
        P(("groups", "row", "rep"), None),
    )
    out_specs = (P(("groups", "row", "rep"), None), P("groups", None), P("groups", None))
    return jax.shard_map(shards, mesh=mesh, in_specs=in_specs, out_specs=out_specs, check_vma=False)
```

```python
import functools

import jax
import jax.numpy as jnp
from jax import lax
from jax.experimental import pallas as pl
from jax.experimental.pallas import tpu as pltpu
from jax.sharding import PartitionSpec as P

F32 = jnp.float32
BF16 = jnp.bfloat16
VMEM = pl.BlockSpec(memory_space=pltpu.VMEM)
SMEM = pl.BlockSpec(memory_space=pltpu.SMEM)
HBM = pl.BlockSpec(memory_space=pltpu.HBM)
MIB = 1 << 20


def dot(a, b, ca=1, cb=0):
    return lax.dot_general(a, b, (((ca,), (cb,)), ((), ())), preferred_element_type=F32)


def densify_kernel(
    blocks, chunks, count_ref, row_hbm, col_hbm, adj_ref, keep_ref, send_ref, tiles, total, rows, cols, sems, small
):
    slots, edge = tiles.shape[0], tiles.shape[1]
    per = slots // chunks
    steps = blocks // 2
    side = jnp.bitwise_and(lax.axis_index("row") + lax.axis_index("rep"), 1)

    def copy(k):
        part = pl.ds(k * per, per)
        return pltpu.make_async_copy(adj_ref.at[part], tiles.at[part], sems.at[k])

    tables = [
        pltpu.make_async_copy(src, dst, small.at[i]) for i, (src, dst) in enumerate(((row_hbm, rows), (col_hbm, cols)))
    ]
    for table in tables:
        table.start()
    for k in range(chunks):
        copy(k).start()

    @pl.loop(0, 2 * blocks)
    def _(i):
        total[i] = jnp.zeros((edge, edge), F32)

    for table in tables:
        table.wait()
    count = count_ref[0]
    for k in range(chunks):
        copy(k).wait()

        @pl.loop(k * per, (k + 1) * per, unroll=4)
        def _(t):
            col = cols[t]
            away = jnp.bitwise_and(col + side, 1)
            where = (away * 2 + rows[t]) * steps + jnp.right_shift(col, 1)
            where = jnp.where(t < count, where, 2 * blocks)
            total[where] += tiles[t].astype(F32)

    @pl.loop(0, steps, unroll=min(steps, 8))
    def _(i):
        at = pl.ds(pl.multiple_of(i * edge, edge), edge)
        for p in range(2):
            send_ref[p, :, at] = total[(2 + p) * steps + i].astype(BF16)
            keep_ref[p, :, at] = total[p * steps + i].astype(BF16)


def densify(tile_row, tile_col, tile_count, adjacency, blocks):
    slots, edge, _ = adjacency.shape
    chunks = 8
    half = jax.ShapeDtypeStruct((2, edge, blocks // 2 * edge), BF16)
    return pl.pallas_call(
        functools.partial(densify_kernel, blocks, chunks),
        out_shape=(half, half),
        in_specs=[SMEM, HBM, HBM, HBM],
        out_specs=(VMEM, VMEM),
        scratch_shapes=[
            pltpu.VMEM((slots, edge, edge), BF16),
            pltpu.VMEM((2 * blocks + 1, edge, edge), F32),
            pltpu.SMEM((slots,), jnp.int32),
            pltpu.SMEM((slots,), jnp.int32),
            pltpu.SemaphoreType.DMA((chunks,)),
            pltpu.SemaphoreType.DMA((2,)),
        ],
        compiler_params=pltpu.CompilerParams(vmem_limit_bytes=48 * MIB),
        cost_estimate=pl.CostEstimate(flops=10**9, bytes_accessed=12 * 10**6, transcendentals=0),
        name="densify",
    )(tile_count, *(pltpu.with_memory_space_constraint(x, pltpu.HBM) for x in (tile_row, tile_col, adjacency)))


def span(start, size):
    return pl.ds(pl.multiple_of(start * size, size), size)


def position(k):
    return jnp.bitwise_xor(jnp.right_shift(lax.axis_index("row"), 1), k)


def terms_kernel(keep_ref, recv_ref, cot_own_ref, cot_other_ref, x_own_ref, x_other_ref, *out_refs):
    nodes, _ = x_own_ref.shape
    classes = cot_own_ref.shape[0]
    rep = lax.axis_index("rep")
    away = 1 - rep
    cot_own, cot_other = cot_own_ref[...], cot_other_ref[...]
    for k, out in enumerate(out_refs):
        at = span(position(k), nodes)
        out[span(rep, nodes), :] = x_own_ref[...]
        out[span(away, nodes), :] = x_other_ref[...]
        for base, a_ref in ((rep, keep_ref), (away, recv_ref)):
            term = dot(cot_own, a_ref[rep, :, at]) + dot(cot_other, a_ref[away, :, at])
            out[pl.ds(pl.multiple_of(2 * nodes + base * classes, 16), classes), :] = term.astype(BF16)


def aggregate_kernel(keep_ref, recv_ref, *refs):
    *x_refs, out_ref = refs
    nodes = keep_ref.shape[1]
    rep = lax.axis_index("rep")
    away = 1 - rep
    parts = [0.0, 0.0]
    back = 0.0
    for k, x_ref in enumerate(x_refs):
        at = span(position(k), nodes)
        x_own, x_other = x_ref[span(rep, nodes), :], x_ref[span(away, nodes), :]
        for p in range(2):
            parts[p] += dot(keep_ref[p, :, at], x_own) + dot(recv_ref[p, :, at], x_other)
        back += x_ref[2 * nodes :, :].astype(F32)
    for p in range(2):
        out_ref[p * nodes : (p + 1) * nodes, :] = parts[p]
    out_ref[2 * nodes :, :] = back


def total_kernel(a_ref, b_ref, o_ref):
    o_ref[...] = (a_ref[...] + b_ref[...]).astype(BF16)


def small_call(kernel, out, name, flops, *args, scratch=()):
    return pl.pallas_call(
        kernel,
        out_shape=out,
        scratch_shapes=scratch,
        in_specs=[VMEM] * len(args),
        out_specs=jax.tree.map(lambda _: VMEM, out),
        compiler_params=pltpu.CompilerParams(vmem_limit_bytes=40 * MIB),
        cost_estimate=pl.CostEstimate(flops=flops, bytes_accessed=10**6, transcendentals=0),
        name=name,
    )(*args)


def local_kernel(keep_ref, recv_ref, win_ref, wout_ref, *refs):
    *x_refs, own_ref, other_ref, grad_ref, stack, proj = refs
    steps = len(x_refs)
    nodes = keep_ref.shape[1]
    width = x_refs[0].shape[1]
    classes = wout_ref.shape[0]
    group = min(steps, 4)
    rep = lax.axis_index("rep")
    away = 1 - rep
    for k, x_ref in enumerate(x_refs):
        stack[position(k)] = x_ref[...]
    own_ref[...] = jnp.zeros_like(own_ref)
    other_ref[...] = jnp.zeros_like(other_ref)
    grad_ref[...] = jnp.zeros_like(grad_ref)

    def body(start):
        rows = pl.ds(start, group)
        agg = jnp.concatenate(
            [stack[rows, c * nodes : (c + 1) * nodes, :].reshape(group * nodes, width) for c in range(2)], axis=0
        )
        base = 2 * nodes
        back = jnp.concatenate(
            [
                stack[start + g, base + c * classes : base + (c + 1) * classes, :]
                for c in range(2)
                for g in range(group)
            ],
            axis=1,
        )
        half = dot(agg, win_ref[...] * 0.5)
        tan = jnp.tanh(half)
        rise = 1.0 + tan
        hidden = (half * rise).astype(BF16)
        gate = rise * (1.0 + half * (1.0 - tan))
        grad_pre = (dot(back, wout_ref[...] * 0.5, 0, 0) * gate).astype(BF16)
        proj[...] = dot(wout_ref[...], hidden, 1, 1).astype(BF16)
        at = pl.ds(pl.multiple_of(start * nodes, nodes), group * nodes)
        mine, theirs = proj[:, span(rep, group * nodes)], proj[:, span(away, group * nodes)]
        for ref, p in ((other_ref, away), (own_ref, rep)):
            ref[...] += dot(mine, keep_ref[p, :, at], 1, 1) + dot(theirs, recv_ref[p, :, at], 1, 1)
        grad_ref[:width, :] += dot(agg, grad_pre, 0, 0)
        grad_ref[width:, :] += dot(back, hidden)

    if group == steps:
        body(0)
    else:
        pl.loop(0, steps, step=group)(body)


def finish_kernel(lo_ref, lr_ref, go_ref, gr_ref, logits_ref, gin_ref, gout_ref):
    width = gin_ref.shape[0]
    logits_ref[...] = lo_ref[...] + lr_ref[...]
    gin_ref[...] = go_ref[:width, :] + gr_ref[:width, :]
    gout_ref[...] = go_ref[width:, :] + gr_ref[width:, :]


def shards(features, adjacency, tile_row, tile_col, tile_count, weight_in, weight_out, cotangent):
    blocks = lax.axis_size("row")
    edge = adjacency.shape[1]
    width = features.shape[1]
    classes = weight_out.shape[1]

    steps = blocks // 2

    def partner(x, k):
        pairs = [(2 * r + p, 2 * (r ^ (2 * k + p)) + p) for r in range(blocks) for p in range(2)]
        return lax.ppermute(x, ("row", "rep"), pairs)

    def swap(x):
        return lax.ppermute(x, "rep", [(0, 1), (1, 0)])

    wout = weight_out.T
    cot = cotangent.T
    hidden = weight_in.shape[1]
    rows = 2 * (edge + classes)

    def like(*shape, dtype=F32):
        return jax.ShapeDtypeStruct(shape, dtype)

    packed = like(rows, width, dtype=BF16)
    keep, send = densify(tile_row, tile_col, tile_count, adjacency, blocks)
    recv = swap(send)
    loads = small_call(
        terms_kernel, (packed,) * steps, "terms", 10**8, keep, recv, cot, swap(cot), features, swap(features)
    )
    arrived = [partner(load, k) for k, load in enumerate(loads)]
    part = small_call(aggregate_kernel, like(rows, width), "aggregate", 10**8, keep, recv, *arrived)
    load = small_call(total_kernel, packed, "total", 10**6, part, swap(part))
    held = [partner(load, k) for k in range(steps)]
    part = like(classes, edge)
    gin, gout = like(width, hidden), like(classes, hidden)
    logit_own, logit_other, grad = small_call(
        local_kernel,
        (part, part, like(width + classes, hidden)),
        "local",
        10**9,
        keep,
        recv,
        weight_in,
        wout,
        *held,
        scratch=[pltpu.VMEM((steps, rows, width), BF16), pltpu.VMEM((classes, 2 * min(steps, 4) * edge), BF16)],
    )
    logits, grad_in, grad_out = small_call(
        finish_kernel, (part, gin, gout), "finish", 10**6, logit_own, swap(logit_other), grad, swap(grad)
    )
    return (logits.T, grad_in, grad_out.T)


def solution(mesh):
    in_specs = (
        P(("groups", "row", "rep"), None),
        P(("groups", "row", "rep"), None, None),
        P(("groups", "row", "rep")),
        P(("groups", "row", "rep")),
        P(("groups", "row", "rep")),
        P(),
        P(),
        P(("groups", "row", "rep"), None),
    )
    out_specs = (P(("groups", "row", "rep"), None), P("groups", None), P("groups", None))
    return jax.shard_map(shards, mesh=mesh, in_specs=in_specs, out_specs=out_specs, check_vma=False)
```

```python
import functools

import jax
import jax.numpy as jnp
from jax import lax
from jax.experimental import pallas as pl
from jax.experimental.pallas import tpu as pltpu
from jax.sharding import PartitionSpec as P

F32 = jnp.float32
BF16 = jnp.bfloat16
VMEM = pl.BlockSpec(memory_space=pltpu.VMEM)
SMEM = pl.BlockSpec(memory_space=pltpu.SMEM)
HBM = pl.BlockSpec(memory_space=pltpu.HBM)
MIB = 1 << 20
FIRST = ((7, 4), (6, 5), (1, 3), (0, 2))
SECOND = FIRST[::-1]


def dot(a, b, ca=1, cb=0):
    return lax.dot_general(a, b, (((ca,), (cb,)), ((), ())), preferred_element_type=F32)


def half_of(block, blocks):
    bits = blocks.bit_length() - 1
    top = block >> (bits - 1)
    return (top ^ (block >> max(bits - 2, 0))) & 1 if bits > 1 else top


def masks_of(pair, blocks):
    steps = blocks // 2
    return [place + steps * (half_of(place, blocks) ^ core) for core, place in enumerate(pair)]


def places(blocks, masks):
    steps = blocks // 2
    if steps != len(masks):
        return [(k, k) for k in range(steps)]
    return [(a % steps, b % steps) for a, b in masks]


def densify_kernel(
    blocks, chunks, count_ref, row_hbm, col_hbm, adj_ref, keep_ref, send_ref, tiles, total, rows, cols, sems, small
):
    slots, edge = tiles.shape[0], tiles.shape[1]
    per = slots // chunks
    steps = blocks // 2
    side = jnp.bitwise_xor(half_of(lax.axis_index("row"), blocks), lax.axis_index("rep"))

    def copy(k):
        part = pl.ds(k * per, per)
        return pltpu.make_async_copy(adj_ref.at[part], tiles.at[part], sems.at[k])

    tables = [
        pltpu.make_async_copy(src, dst, small.at[i]) for i, (src, dst) in enumerate(((row_hbm, rows), (col_hbm, cols)))
    ]
    for table in tables:
        table.start()
    for k in range(chunks):
        copy(k).start()

    @pl.loop(0, 2 * blocks)
    def _(i):
        total[i] = jnp.zeros((edge, edge), F32)

    for table in tables:
        table.wait()
    count = count_ref[0]
    for k in range(chunks):
        copy(k).wait()

        @pl.loop(k * per, (k + 1) * per, unroll=4)
        def _(t):
            col = cols[t]
            away = jnp.bitwise_xor(half_of(col, blocks), side)
            where = (away * 2 + rows[t]) * steps + jnp.bitwise_and(col, steps - 1)
            where = jnp.where(t < count, where, 2 * blocks)
            total[where] += tiles[t].astype(F32)

    @pl.loop(0, steps, unroll=min(steps, 8))
    def _(i):
        at = pl.ds(pl.multiple_of(i * edge, edge), edge)
        for p in range(2):
            send_ref[p, :, at] = total[(2 + p) * steps + i].astype(BF16)
            keep_ref[p, :, at] = total[p * steps + i].astype(BF16)


def densify(tile_row, tile_col, tile_count, adjacency, blocks):
    slots, edge, _ = adjacency.shape
    chunks = 8
    half = jax.ShapeDtypeStruct((2, edge, blocks // 2 * edge), BF16)
    return pl.pallas_call(
        functools.partial(densify_kernel, blocks, chunks),
        out_shape=(half, half),
        in_specs=[SMEM, HBM, HBM, HBM],
        out_specs=(VMEM, VMEM),
        scratch_shapes=[
            pltpu.VMEM((slots, edge, edge), BF16),
            pltpu.VMEM((2 * blocks + 1, edge, edge), F32),
            pltpu.SMEM((slots,), jnp.int32),
            pltpu.SMEM((slots,), jnp.int32),
            pltpu.SemaphoreType.DMA((chunks,)),
            pltpu.SemaphoreType.DMA((2,)),
        ],
        compiler_params=pltpu.CompilerParams(vmem_limit_bytes=48 * MIB),
        cost_estimate=pl.CostEstimate(flops=10**9, bytes_accessed=12 * 10**6, transcendentals=0),
        name="densify",
    )(tile_count, *(pltpu.with_memory_space_constraint(x, pltpu.HBM) for x in (tile_row, tile_col, adjacency)))


def span(start, size):
    return pl.ds(pl.multiple_of(start * size, size), size)


def position(steps, pair):
    which = jnp.where(lax.axis_index("rep") == 0, pair[0], pair[1])
    return jnp.bitwise_xor(jnp.bitwise_and(lax.axis_index("row"), steps - 1), which)


def terms_kernel(order, keep_ref, recv_ref, cot_own_ref, cot_other_ref, x_own_ref, x_other_ref, *out_refs):
    nodes, _ = x_own_ref.shape
    classes = cot_own_ref.shape[0]
    rep = lax.axis_index("rep")
    away = 1 - rep
    cot_own, cot_other = cot_own_ref[...], cot_other_ref[...]
    for k, out in enumerate(out_refs):
        at = span(position(len(order), order[k]), nodes)
        out[span(rep, nodes), :] = x_own_ref[...]
        out[span(away, nodes), :] = x_other_ref[...]
        for base, a_ref in ((rep, keep_ref), (away, recv_ref)):
            term = dot(cot_own, a_ref[rep, :, at]) + dot(cot_other, a_ref[away, :, at])
            out[pl.ds(pl.multiple_of(2 * nodes + base * classes, 16), classes), :] = term.astype(BF16)


def aggregate_kernel(order, keep_ref, recv_ref, *refs):
    *x_refs, out_ref = refs
    nodes = keep_ref.shape[1]
    rep = lax.axis_index("rep")
    away = 1 - rep
    parts = [0.0, 0.0]
    back = 0.0
    for k, x_ref in enumerate(x_refs):
        at = span(position(len(order), order[k]), nodes)
        x_own, x_other = x_ref[span(rep, nodes), :], x_ref[span(away, nodes), :]
        for p in range(2):
            parts[p] += dot(keep_ref[p, :, at], x_own) + dot(recv_ref[p, :, at], x_other)
        back += x_ref[2 * nodes :, :].astype(F32)
    for p in range(2):
        out_ref[p * nodes : (p + 1) * nodes, :] = parts[p]
    out_ref[2 * nodes :, :] = back


def total_kernel(a_ref, b_ref, o_ref):
    o_ref[...] = (a_ref[...] + b_ref[...]).astype(BF16)


def small_call(kernel, out, name, flops, *args, scratch=()):
    return pl.pallas_call(
        kernel,
        out_shape=out,
        scratch_shapes=scratch,
        in_specs=[VMEM] * len(args),
        out_specs=jax.tree.map(lambda _: VMEM, out),
        compiler_params=pltpu.CompilerParams(vmem_limit_bytes=40 * MIB),
        cost_estimate=pl.CostEstimate(flops=flops, bytes_accessed=10**6, transcendentals=0),
        name=name,
    )(*args)


def local_kernel(order, keep_ref, recv_ref, win_ref, wout_ref, *refs):
    *x_refs, own_ref, other_ref, grad_ref, stack, proj = refs
    steps = len(x_refs)
    nodes = keep_ref.shape[1]
    width = x_refs[0].shape[1]
    classes = wout_ref.shape[0]
    group = min(steps, 4)
    rep = lax.axis_index("rep")
    away = 1 - rep
    for k, x_ref in enumerate(x_refs):
        stack[position(steps, order[k])] = x_ref[...]
    own_ref[...] = jnp.zeros_like(own_ref)
    other_ref[...] = jnp.zeros_like(other_ref)
    grad_ref[...] = jnp.zeros_like(grad_ref)

    def body(start):
        rows = pl.ds(start, group)
        agg = jnp.concatenate(
            [stack[rows, c * nodes : (c + 1) * nodes, :].reshape(group * nodes, width) for c in range(2)], axis=0
        )
        base = 2 * nodes
        back = jnp.concatenate(
            [
                stack[start + g, base + c * classes : base + (c + 1) * classes, :]
                for c in range(2)
                for g in range(group)
            ],
            axis=1,
        )
        half = dot(agg, win_ref[...] * 0.5)
        tan = jnp.tanh(half)
        rise = 1.0 + tan
        hidden = (half * rise).astype(BF16)
        gate = rise * (1.0 + half * (1.0 - tan))
        grad_pre = (dot(back, wout_ref[...] * 0.5, 0, 0) * gate).astype(BF16)
        proj[...] = dot(wout_ref[...], hidden, 1, 1).astype(BF16)
        at = pl.ds(pl.multiple_of(start * nodes, nodes), group * nodes)
        mine, theirs = proj[:, span(rep, group * nodes)], proj[:, span(away, group * nodes)]
        for ref, p in ((other_ref, away), (own_ref, rep)):
            ref[...] += dot(mine, keep_ref[p, :, at], 1, 1) + dot(theirs, recv_ref[p, :, at], 1, 1)
        grad_ref[:width, :] += dot(agg, grad_pre, 0, 0)
        grad_ref[width:, :] += dot(back, hidden)

    if group == steps:
        body(0)
    else:
        pl.loop(0, steps, step=group)(body)


def finish_kernel(lo_ref, lr_ref, go_ref, gr_ref, logits_ref, gin_ref, gout_ref):
    width = gin_ref.shape[0]
    logits_ref[...] = lo_ref[...] + lr_ref[...]
    gin_ref[...] = go_ref[:width, :] + gr_ref[:width, :]
    gout_ref[...] = go_ref[width:, :] + gr_ref[width:, :]


def shards(features, adjacency, tile_row, tile_col, tile_count, weight_in, weight_out, cotangent):
    blocks = lax.axis_size("row")
    edge = adjacency.shape[1]
    width = features.shape[1]
    classes = weight_out.shape[1]

    steps = blocks // 2

    first, second = places(blocks, FIRST), places(blocks, SECOND)

    def partner(x, pair):
        masks = masks_of(pair, blocks)
        pairs = [(2 * r + p, 2 * (r ^ masks[p]) + p) for r in range(blocks) for p in range(2)]
        return lax.ppermute(x, ("row", "rep"), pairs)

    def swap(x):
        return lax.ppermute(x, "rep", [(0, 1), (1, 0)])

    wout = weight_out.T
    cot = cotangent.T
    hidden = weight_in.shape[1]
    rows = 2 * (edge + classes)

    def like(*shape, dtype=F32):
        return jax.ShapeDtypeStruct(shape, dtype)

    packed = like(rows, width, dtype=BF16)
    keep, send = densify(tile_row, tile_col, tile_count, adjacency, blocks)
    recv = swap(send)
    loads = small_call(
        functools.partial(terms_kernel, first), (packed,) * steps, "terms", 10**8, keep, recv, cot, swap(cot), features, swap(features)
    )
    arrived = [partner(load, pair) for load, pair in zip(loads, first)]
    part = small_call(functools.partial(aggregate_kernel, first), like(rows, width), "aggregate", 10**8, keep, recv, *arrived)
    load = small_call(total_kernel, packed, "total", 10**6, part, swap(part))
    held = [partner(load, pair) for pair in second]
    part = like(classes, edge)
    gin, gout = like(width, hidden), like(classes, hidden)
    logit_own, logit_other, grad = small_call(
        functools.partial(local_kernel, second),
        (part, part, like(width + classes, hidden)),
        "local",
        10**9,
        keep,
        recv,
        weight_in,
        wout,
        *held,
        scratch=[pltpu.VMEM((steps, rows, width), BF16), pltpu.VMEM((classes, 2 * min(steps, 4) * edge), BF16)],
    )
    logits, grad_in, grad_out = small_call(
        finish_kernel, (part, gin, gout), "finish", 10**6, logit_own, swap(logit_other), grad, swap(grad)
    )
    return (logits.T, grad_in, grad_out.T)


def solution(mesh):
    in_specs = (
        P(("groups", "row", "rep"), None),
        P(("groups", "row", "rep"), None, None),
        P(("groups", "row", "rep")),
        P(("groups", "row", "rep")),
        P(("groups", "row", "rep")),
        P(),
        P(),
        P(("groups", "row", "rep"), None),
    )
    out_specs = (P(("groups", "row", "rep"), None), P("groups", None), P("groups", None))
    return jax.shard_map(shards, mesh=mesh, in_specs=in_specs, out_specs=out_specs, check_vma=False)
```

```python
import functools

import jax
import jax.numpy as jnp
from jax import lax
from jax.experimental import pallas as pl
from jax.experimental.pallas import tpu as pltpu
from jax.sharding import PartitionSpec as P

F32 = jnp.float32
BF16 = jnp.bfloat16
VMEM = pl.BlockSpec(memory_space=pltpu.VMEM)
SMEM = pl.BlockSpec(memory_space=pltpu.SMEM)
HBM = pl.BlockSpec(memory_space=pltpu.HBM)
MIB = 1 << 20
FIRST = ((7, 4), (6, 5), (1, 3), (0, 2))
SECOND = ((0, 2), (1, 3), (6, 4), (7, 5))
LATE = 3


def dot(a, b, ca=1, cb=0):
    return lax.dot_general(a, b, (((ca,), (cb,)), ((), ())), preferred_element_type=F32)


def half_of(block, blocks):
    bits = blocks.bit_length() - 1
    top = block >> (bits - 1)
    return (top ^ (block >> max(bits - 2, 0))) & 1 if bits > 1 else top


def masks_of(pair, blocks):
    steps = blocks // 2
    return [place + steps * (half_of(place, blocks) ^ core) for core, place in enumerate(pair)]


def places(blocks, masks):
    steps = blocks // 2
    if steps != len(masks):
        return [(k, k) for k in range(steps)]
    return [(a % steps, b % steps) for a, b in masks]


def densify_kernel(
    blocks, chunks, count_ref, row_hbm, col_hbm, adj_ref, keep_ref, send_ref, tiles, total, rows, cols, sems, small
):
    slots, edge = tiles.shape[0], tiles.shape[1]
    per = slots // chunks
    steps = blocks // 2
    side = jnp.bitwise_xor(half_of(lax.axis_index("row"), blocks), lax.axis_index("rep"))

    def copy(k):
        part = pl.ds(k * per, per)
        return pltpu.make_async_copy(adj_ref.at[part], tiles.at[part], sems.at[k])

    tables = [
        pltpu.make_async_copy(src, dst, small.at[i]) for i, (src, dst) in enumerate(((row_hbm, rows), (col_hbm, cols)))
    ]
    for table in tables:
        table.start()
    for k in range(chunks):
        copy(k).start()

    @pl.loop(0, 2 * blocks)
    def _(i):
        total[i] = jnp.zeros((edge, edge), F32)

    for table in tables:
        table.wait()
    count = count_ref[0]
    for k in range(chunks):
        copy(k).wait()

        @pl.loop(k * per, (k + 1) * per, unroll=4)
        def _(t):
            col = cols[t]
            away = jnp.bitwise_xor(half_of(col, blocks), side)
            where = (away * 2 + rows[t]) * steps + jnp.bitwise_and(col, steps - 1)
            where = jnp.where(t < count, where, 2 * blocks)
            total[where] += tiles[t].astype(F32)

    @pl.loop(0, steps, unroll=min(steps, 8))
    def _(i):
        at = pl.ds(pl.multiple_of(i * edge, edge), edge)
        for p in range(2):
            send_ref[p, :, at] = total[(2 + p) * steps + i].astype(BF16)
            keep_ref[p, :, at] = total[p * steps + i].astype(BF16)


def densify(tile_row, tile_col, tile_count, adjacency, blocks):
    slots, edge, _ = adjacency.shape
    chunks = 8
    half = jax.ShapeDtypeStruct((2, edge, blocks // 2 * edge), BF16)
    return pl.pallas_call(
        functools.partial(densify_kernel, blocks, chunks),
        out_shape=(half, half),
        in_specs=[SMEM, HBM, HBM, HBM],
        out_specs=(VMEM, VMEM),
        scratch_shapes=[
            pltpu.VMEM((slots, edge, edge), BF16),
            pltpu.VMEM((2 * blocks + 1, edge, edge), F32),
            pltpu.SMEM((slots,), jnp.int32),
            pltpu.SMEM((slots,), jnp.int32),
            pltpu.SemaphoreType.DMA((chunks,)),
            pltpu.SemaphoreType.DMA((2,)),
        ],
        compiler_params=pltpu.CompilerParams(vmem_limit_bytes=48 * MIB),
        cost_estimate=pl.CostEstimate(flops=10**9, bytes_accessed=12 * 10**6, transcendentals=0),
        name="densify",
    )(tile_count, *(pltpu.with_memory_space_constraint(x, pltpu.HBM) for x in (tile_row, tile_col, adjacency)))


def span(start, size):
    return pl.ds(pl.multiple_of(start * size, size), size)


def position(steps, pair):
    which = jnp.where(lax.axis_index("rep") == 0, pair[0], pair[1])
    return jnp.bitwise_xor(jnp.bitwise_and(lax.axis_index("row"), steps - 1), which)


def terms_kernel(order, keep_ref, recv_ref, cot_own_ref, cot_other_ref, x_own_ref, x_other_ref, *out_refs):
    nodes, _ = x_own_ref.shape
    classes = cot_own_ref.shape[0]
    rep = lax.axis_index("rep")
    away = 1 - rep
    cot_own, cot_other = cot_own_ref[...], cot_other_ref[...]
    for k, out in enumerate(out_refs):
        at = span(position(len(order), order[k]), nodes)
        out[span(rep, nodes), :] = x_own_ref[...]
        out[span(away, nodes), :] = x_other_ref[...]
        for base, a_ref in ((rep, keep_ref), (away, recv_ref)):
            term = dot(cot_own, a_ref[rep, :, at]) + dot(cot_other, a_ref[away, :, at])
            out[pl.ds(pl.multiple_of(2 * nodes + base * classes, 16), classes), :] = term.astype(BF16)


def aggregate_kernel(order, keep_ref, recv_ref, *refs):
    *x_refs, out_ref = refs
    nodes = keep_ref.shape[1]
    rep = lax.axis_index("rep")
    away = 1 - rep
    parts = [0.0, 0.0]
    back = 0.0
    for k, x_ref in enumerate(x_refs):
        at = span(position(len(order), order[k]), nodes)
        x_own, x_other = x_ref[span(rep, nodes), :], x_ref[span(away, nodes), :]
        for p in range(2):
            parts[p] += dot(keep_ref[p, :, at], x_own) + dot(recv_ref[p, :, at], x_other)
        back += x_ref[2 * nodes :, :].astype(F32)
    for p in range(2):
        out_ref[p * nodes : (p + 1) * nodes, :] = parts[p]
    out_ref[2 * nodes :, :] = back


def total_kernel(a_ref, b_ref, o_ref):
    o_ref[...] = (a_ref[...] + b_ref[...]).astype(BF16)


def small_call(kernel, out, name, flops, *args, scratch=()):
    return pl.pallas_call(
        kernel,
        out_shape=out,
        scratch_shapes=scratch,
        in_specs=[VMEM] * len(args),
        out_specs=jax.tree.map(lambda _: VMEM, out),
        compiler_params=pltpu.CompilerParams(vmem_limit_bytes=44 * MIB),
        cost_estimate=pl.CostEstimate(flops=flops, bytes_accessed=10**6, transcendentals=0),
        name=name,
    )(*args)


def block_terms(place, x_ref, keep_ref, recv_ref, win_ref, wout_ref, own_ref, other_ref, proj):
    nodes = keep_ref.shape[1]
    classes = wout_ref.shape[0]
    rep = lax.axis_index("rep")
    away = 1 - rep
    agg = x_ref[: 2 * nodes, :]
    back = jnp.concatenate([x_ref[2 * nodes : 2 * nodes + classes, :], x_ref[2 * nodes + classes :, :]], axis=1)
    half = dot(agg, win_ref[...] * 0.5)
    tan = jnp.tanh(half)
    rise = 1.0 + tan
    hidden = (half * rise).astype(BF16)
    gate = rise * (1.0 + half * (1.0 - tan))
    grad_pre = (dot(back, wout_ref[...] * 0.5, 0, 0) * gate).astype(BF16)
    proj[...] = dot(wout_ref[...], hidden, 1, 1).astype(BF16)
    mine, theirs = proj[:, span(rep, nodes)], proj[:, span(away, nodes)]
    at = span(place, nodes)
    for ref, p in ((other_ref, away), (own_ref, rep)):
        ref[...] += dot(mine, keep_ref[p, :, at], 1, 1) + dot(theirs, recv_ref[p, :, at], 1, 1)
    return dot(agg, grad_pre, 0, 0), dot(back, hidden)


def early_kernel(places, keep_ref, recv_ref, win_ref, wout_ref, *refs):
    *x_refs, own_ref, other_ref, grads_ref, proj = refs
    steps = grads_ref.shape[0]
    width = win_ref.shape[0]
    own_ref[...] = jnp.zeros_like(own_ref)
    other_ref[...] = jnp.zeros_like(other_ref)
    for x_ref, pair in zip(x_refs, places):
        place = position(steps, pair)
        gin, gout = block_terms(place, x_ref, keep_ref, recv_ref, win_ref, wout_ref, own_ref, other_ref, proj)
        grads_ref[place, :width, :] = gin
        grads_ref[place, width:, :] = gout


def late_kernel(pair, keep_ref, recv_ref, win_ref, wout_ref, x_ref, own_in, other_in, grads_ref, *refs):
    own_ref, other_ref, grad_ref, last, proj = refs
    steps = grads_ref.shape[0]
    width = win_ref.shape[0]
    own_ref[...] = own_in[...]
    other_ref[...] = other_in[...]
    place = position(steps, pair)
    gin, gout = block_terms(place, x_ref, keep_ref, recv_ref, win_ref, wout_ref, own_ref, other_ref, proj)
    last[:width, :] = gin
    last[width:, :] = gout
    grad_ref[...] = jnp.where(place == 0, last[...], grads_ref[0])
    for i in range(1, steps):
        grad_ref[...] += jnp.where(place == i, last[...], grads_ref[i])


def finish_kernel(lo_ref, lr_ref, go_ref, gr_ref, logits_ref, gin_ref, gout_ref):
    width = gin_ref.shape[0]
    logits_ref[...] = lo_ref[...] + lr_ref[...]
    gin_ref[...] = go_ref[:width, :] + gr_ref[:width, :]
    gout_ref[...] = go_ref[width:, :] + gr_ref[width:, :]


def shards(features, adjacency, tile_row, tile_col, tile_count, weight_in, weight_out, cotangent):
    blocks = lax.axis_size("row")
    edge = adjacency.shape[1]
    width = features.shape[1]
    classes = weight_out.shape[1]

    steps = blocks // 2

    first, second = places(blocks, FIRST), places(blocks, SECOND)

    def partner(x, pair, masks=None):
        masks = masks or masks_of(pair, blocks)
        pairs = [(2 * r + p, 2 * (r ^ masks[p]) + p) for r in range(blocks) for p in range(2)]
        return lax.ppermute(x, ("row", "rep"), pairs)

    def swap(x):
        return lax.ppermute(x, "rep", [(0, 1), (1, 0)])

    wout = weight_out.T
    cot = cotangent.T
    hidden = weight_in.shape[1]
    rows = 2 * (edge + classes)

    def like(*shape, dtype=F32):
        return jax.ShapeDtypeStruct(shape, dtype)

    packed = like(rows, width, dtype=BF16)
    keep, send = densify(tile_row, tile_col, tile_count, adjacency, blocks)
    recv = swap(send)
    loads = small_call(
        functools.partial(terms_kernel, first), (packed,) * steps, "terms", 10**8, keep, recv, cot, swap(cot), features, swap(features)
    )
    arrived = [partner(load, pair) for load, pair in zip(loads, first)]
    part = small_call(functools.partial(aggregate_kernel, first), like(rows, width), "aggregate", 10**8, keep, recv, *arrived)
    load = small_call(total_kernel, packed, "total", 10**6, part, swap(part))
    if steps == len(SECOND):
        held = [partner(load, pair) for pair in second[:3]]
        held.append(partner(held[2], None, (1, 1)))
    else:
        held = [partner(load, pair) for pair in second]
    part = like(classes, edge)
    gin, gout = like(width, hidden), like(classes, hidden)
    late = LATE if steps == len(SECOND) else steps - 1
    early = [k for k in range(steps) if k != late]
    weights = (keep, recv, weight_in, wout)
    proj = pltpu.VMEM((classes, 2 * edge), BF16)
    sums = small_call(
        functools.partial(early_kernel, [second[k] for k in early]),
        (part, part, like(steps, width + classes, hidden)),
        "early",
        10**8,
        *weights,
        *(held[k] for k in early),
        scratch=[proj],
    )
    logit_own, logit_other, grad = small_call(
        functools.partial(late_kernel, second[late]),
        (part, part, like(width + classes, hidden)),
        "late",
        10**8,
        *weights,
        held[late],
        *sums,
        scratch=[pltpu.VMEM((width + classes, hidden), F32), proj],
    )
    logits, grad_in, grad_out = small_call(
        finish_kernel, (part, gin, gout), "finish", 10**6, logit_own, swap(logit_other), grad, swap(grad)
    )
    return (logits.T, grad_in, grad_out.T)


def solution(mesh):
    in_specs = (
        P(("groups", "row", "rep"), None),
        P(("groups", "row", "rep"), None, None),
        P(("groups", "row", "rep")),
        P(("groups", "row", "rep")),
        P(("groups", "row", "rep")),
        P(),
        P(),
        P(("groups", "row", "rep"), None),
    )
    out_specs = (P(("groups", "row", "rep"), None), P("groups", None), P("groups", None))
    return jax.shard_map(shards, mesh=mesh, in_specs=in_specs, out_specs=out_specs, check_vma=False)
```

```python
import functools

import jax
import jax.numpy as jnp
from jax import lax
from jax.experimental import pallas as pl
from jax.experimental.pallas import tpu as pltpu
from jax.sharding import PartitionSpec as P

F32 = jnp.float32
BF16 = jnp.bfloat16
VMEM = pl.BlockSpec(memory_space=pltpu.VMEM)
SMEM = pl.BlockSpec(memory_space=pltpu.SMEM)
HBM = pl.BlockSpec(memory_space=pltpu.HBM)
MIB = 1 << 20
FIRST = ((7, 4), (6, 5), (1, 3), (0, 2))
SECOND = ((0, 2), (1, 3), (6, 4), (7, 5))
LATE = 3
PIECE = 16


def dot(a, b, ca=1, cb=0):
    return lax.dot_general(a, b, (((ca,), (cb,)), ((), ())), preferred_element_type=F32)


def half_of(block, blocks):
    bits = blocks.bit_length() - 1
    top = block >> (bits - 1)
    return (top ^ (block >> max(bits - 2, 0))) & 1 if bits > 1 else top


def masks_of(pair, blocks):
    steps = blocks // 2
    return [place + steps * (half_of(place, blocks) ^ core) for core, place in enumerate(pair)]


def places(blocks, masks):
    steps = blocks // 2
    if steps != len(masks):
        return [(k, k) for k in range(steps)]
    return [(a % steps, b % steps) for a, b in masks]


def densify_kernel(
    blocks, chunks, count_ref, row_hbm, col_hbm, adj_ref, keep_ref, send_ref, tiles, total, rows, cols, sems, small
):
    slots, edge = tiles.shape[0], tiles.shape[1]
    per = slots // chunks
    steps = blocks // 2
    side = jnp.bitwise_xor(half_of(lax.axis_index("row"), blocks), lax.axis_index("rep"))

    def copy(k):
        part = pl.ds(k * per, per)
        return pltpu.make_async_copy(adj_ref.at[part], tiles.at[part], sems.at[k])

    tables = [
        pltpu.make_async_copy(src, dst, small.at[i]) for i, (src, dst) in enumerate(((row_hbm, rows), (col_hbm, cols)))
    ]
    for table in tables:
        table.start()
    for k in range(chunks):
        copy(k).start()

    @pl.loop(0, 2 * blocks)
    def _(i):
        total[i] = jnp.zeros((edge, edge), F32)

    for table in tables:
        table.wait()
    count = count_ref[0]
    for k in range(chunks):
        copy(k).wait()

        @pl.loop(k * per, (k + 1) * per, unroll=4)
        def _(t):
            col = cols[t]
            away = jnp.bitwise_xor(half_of(col, blocks), side)
            where = (away * 2 + rows[t]) * steps + jnp.bitwise_and(col, steps - 1)
            where = jnp.where(t < count, where, 2 * blocks)
            total[where] += tiles[t].astype(F32)

    @pl.loop(0, steps, unroll=min(steps, 8))
    def _(i):
        at = pl.ds(pl.multiple_of(i * edge, edge), edge)
        for p in range(2):
            send_ref[p, :, at] = total[(2 + p) * steps + i].astype(BF16)
            keep_ref[p, :, at] = total[p * steps + i].astype(BF16)


def densify(tile_row, tile_col, tile_count, adjacency, blocks):
    slots, edge, _ = adjacency.shape
    chunks = 8
    half = jax.ShapeDtypeStruct((2, edge, blocks // 2 * edge), BF16)
    return pl.pallas_call(
        functools.partial(densify_kernel, blocks, chunks),
        out_shape=(half, half),
        in_specs=[SMEM, HBM, HBM, HBM],
        out_specs=(VMEM, VMEM),
        scratch_shapes=[
            pltpu.VMEM((slots, edge, edge), BF16),
            pltpu.VMEM((2 * blocks + 1, edge, edge), F32),
            pltpu.SMEM((slots,), jnp.int32),
            pltpu.SMEM((slots,), jnp.int32),
            pltpu.SemaphoreType.DMA((chunks,)),
            pltpu.SemaphoreType.DMA((2,)),
        ],
        compiler_params=pltpu.CompilerParams(vmem_limit_bytes=48 * MIB),
        cost_estimate=pl.CostEstimate(flops=10**9, bytes_accessed=12 * 10**6, transcendentals=0),
        name="densify",
    )(tile_count, *(pltpu.with_memory_space_constraint(x, pltpu.HBM) for x in (tile_row, tile_col, adjacency)))


def span(start, size):
    return pl.ds(pl.multiple_of(start * size, size), size)


def position(steps, pair):
    which = jnp.where(lax.axis_index("rep") == 0, pair[0], pair[1])
    return jnp.bitwise_xor(jnp.bitwise_and(lax.axis_index("row"), steps - 1), which)


def terms_kernel(order, keep_ref, recv_ref, cot_own_ref, cot_other_ref, x_own_ref, x_other_ref, *out_refs):
    nodes, _ = x_own_ref.shape
    classes = cot_own_ref.shape[0]
    rep = lax.axis_index("rep")
    away = 1 - rep
    cot_own, cot_other = cot_own_ref[...], cot_other_ref[...]
    for k, out in enumerate(out_refs):
        at = span(position(len(order), order[k]), nodes)
        out[span(rep, nodes), :] = x_own_ref[...]
        out[span(away, nodes), :] = x_other_ref[...]
        for base, a_ref in ((rep, keep_ref), (away, recv_ref)):
            term = dot(cot_own, a_ref[rep, :, at]) + dot(cot_other, a_ref[away, :, at])
            out[pl.ds(pl.multiple_of(2 * nodes + base * classes, 16), classes), :] = term.astype(BF16)


def aggregate_kernel(order, keep_ref, recv_ref, *refs):
    *x_refs, out_ref = refs
    nodes = keep_ref.shape[1]
    rep = lax.axis_index("rep")
    away = 1 - rep
    parts = [0.0, 0.0]
    back = 0.0
    for k, x_ref in enumerate(x_refs):
        at = span(position(len(order), order[k]), nodes)
        x_own, x_other = x_ref[span(rep, nodes), :], x_ref[span(away, nodes), :]
        for p in range(2):
            parts[p] += dot(keep_ref[p, :, at], x_own) + dot(recv_ref[p, :, at], x_other)
        back += x_ref[2 * nodes :, :].astype(F32)
    for p in range(2):
        out_ref[p * nodes : (p + 1) * nodes, :] = parts[p]
    out_ref[2 * nodes :, :] = back


def total_kernel(a_ref, b_ref, o_ref):
    o_ref[...] = (a_ref[...] + b_ref[...]).astype(BF16)


def small_call(kernel, out, name, flops, *args, scratch=()):
    return pl.pallas_call(
        kernel,
        out_shape=out,
        scratch_shapes=scratch,
        in_specs=[VMEM] * len(args),
        out_specs=jax.tree.map(lambda _: VMEM, out),
        compiler_params=pltpu.CompilerParams(vmem_limit_bytes=44 * MIB),
        cost_estimate=pl.CostEstimate(flops=flops, bytes_accessed=10**6, transcendentals=0),
        name=name,
    )(*args)


def block_terms(place, x_ref, keep_ref, recv_ref, win_ref, wout_ref, own_ref, other_ref, proj):
    nodes = keep_ref.shape[1]
    classes = wout_ref.shape[0]
    rep = lax.axis_index("rep")
    away = 1 - rep
    agg = x_ref[: 2 * nodes, :]
    back = jnp.concatenate([x_ref[2 * nodes : 2 * nodes + classes, :], x_ref[2 * nodes + classes :, :]], axis=1)
    half = dot(agg, win_ref[...] * 0.5)
    tan = jnp.tanh(half)
    rise = 1.0 + tan
    hidden = (half * rise).astype(BF16)
    gate = rise * (1.0 + half * (1.0 - tan))
    grad_pre = (dot(back, wout_ref[...] * 0.5, 0, 0) * gate).astype(BF16)
    proj[...] = dot(wout_ref[...], hidden, 1, 1).astype(BF16)
    mine, theirs = proj[:, span(rep, nodes)], proj[:, span(away, nodes)]
    at = span(place, nodes)
    for ref, p in ((other_ref, away), (own_ref, rep)):
        ref[...] += dot(mine, keep_ref[p, :, at], 1, 1) + dot(theirs, recv_ref[p, :, at], 1, 1)
    return dot(agg, grad_pre, 0, 0), dot(back, hidden)


def early_kernel(places, keep_ref, recv_ref, win_ref, wout_ref, *refs):
    *x_refs, own_ref, other_ref, grads_ref, proj = refs
    steps = grads_ref.shape[0]
    width = win_ref.shape[0]
    own_ref[...] = jnp.zeros_like(own_ref)
    other_ref[...] = jnp.zeros_like(other_ref)
    for x_ref, pair in zip(x_refs, places):
        place = position(steps, pair)
        gin, gout = block_terms(place, x_ref, keep_ref, recv_ref, win_ref, wout_ref, own_ref, other_ref, proj)
        grads_ref[place, :width, :] = gin
        grads_ref[place, width:, :] = gout


def late_kernel(pair, keep_ref, recv_ref, win_ref, wout_ref, x_ref, own_in, other_in, grads_ref, *refs):
    own_ref, grad_ref, other_ref, last, proj = refs
    steps, rows, _ = grads_ref.shape
    width = win_ref.shape[0]
    nodes = own_ref.shape[1]
    own_ref[...] = own_in[...]
    other_ref[...] = other_in[...]
    place = position(steps, pair)
    gin, gout = block_terms(place, x_ref, keep_ref, recv_ref, win_ref, wout_ref, own_ref, other_ref, proj)
    last[:width, :] = gin
    last[width:, :] = gout
    total = jnp.where(place == 0, last[...], grads_ref[0])
    for i in range(1, steps):
        total += jnp.where(place == i, last[...], grads_ref[i])
    grad_ref[:rows, :] = total.astype(BF16)
    grad_ref[rows:, :] = jnp.zeros_like(grad_ref[rows:, :])
    for i in range(other_ref.shape[0] // PIECE):
        grad_ref[rows:, i * nodes : (i + 1) * nodes] = other_ref[i * PIECE : (i + 1) * PIECE, :].astype(BF16)


def finish_kernel(lo_ref, go_ref, gr_ref, logits_ref, gin_ref, gout_ref):
    width = gin_ref.shape[0]
    classes, nodes = logits_ref.shape
    rows = width + classes
    for i in range(classes // PIECE):
        at = slice(i * PIECE, (i + 1) * PIECE)
        logits_ref[at, :] = lo_ref[at, :] + gr_ref[rows:, i * nodes : (i + 1) * nodes].astype(F32)
    gin_ref[...] = go_ref[:width, :].astype(F32) + gr_ref[:width, :].astype(F32)
    gout_ref[...] = go_ref[width:rows, :].astype(F32) + gr_ref[width:rows, :].astype(F32)


def shards(features, adjacency, tile_row, tile_col, tile_count, weight_in, weight_out, cotangent):
    blocks = lax.axis_size("row")
    edge = adjacency.shape[1]
    width = features.shape[1]
    classes = weight_out.shape[1]

    steps = blocks // 2

    first, second = places(blocks, FIRST), places(blocks, SECOND)

    def partner(x, pair, masks=None):
        masks = masks or masks_of(pair, blocks)
        pairs = [(2 * r + p, 2 * (r ^ masks[p]) + p) for r in range(blocks) for p in range(2)]
        return lax.ppermute(x, ("row", "rep"), pairs)

    def swap(x):
        return lax.ppermute(x, "rep", [(0, 1), (1, 0)])

    wout = weight_out.T
    cot = cotangent.T
    hidden = weight_in.shape[1]
    rows = 2 * (edge + classes)

    def like(*shape, dtype=F32):
        return jax.ShapeDtypeStruct(shape, dtype)

    packed = like(rows, width, dtype=BF16)
    keep, send = densify(tile_row, tile_col, tile_count, adjacency, blocks)
    recv = swap(send)
    loads = small_call(
        functools.partial(terms_kernel, first), (packed,) * steps, "terms", 10**8, keep, recv, cot, swap(cot), features, swap(features)
    )
    arrived = [partner(load, pair) for load, pair in zip(loads, first)]
    part = small_call(functools.partial(aggregate_kernel, first), like(rows, width), "aggregate", 10**8, keep, recv, *arrived)
    load = small_call(total_kernel, packed, "total", 10**6, part, swap(part))
    if steps == len(SECOND):
        held = [partner(load, pair) for pair in second[:3]]
        held.append(partner(held[2], None, (1, 1)))
    else:
        held = [partner(load, pair) for pair in second]
    part = like(classes, edge)
    gin, gout = like(width, hidden), like(classes, hidden)
    late = LATE if steps == len(SECOND) else steps - 1
    early = [k for k in range(steps) if k != late]
    weights = (keep, recv, weight_in, wout)
    proj = pltpu.VMEM((classes, 2 * edge), BF16)
    sums = small_call(
        functools.partial(early_kernel, [second[k] for k in early]),
        (part, part, like(steps, width + classes, hidden)),
        "early",
        10**8,
        *weights,
        *(held[k] for k in early),
        scratch=[proj],
    )
    logit_own, grad = small_call(
        functools.partial(late_kernel, second[late]),
        (part, like(width + classes + PIECE, hidden, dtype=BF16)),
        "late",
        10**8,
        *weights,
        held[late],
        *sums,
        scratch=[pltpu.VMEM(part.shape, F32), pltpu.VMEM((width + classes, hidden), F32), proj],
    )
    logits, grad_in, grad_out = small_call(
        finish_kernel, (part, gin, gout), "finish", 10**6, logit_own, grad, swap(grad)
    )
    return (logits.T, grad_in, grad_out.T)


def solution(mesh):
    in_specs = (
        P(("groups", "row", "rep"), None),
        P(("groups", "row", "rep"), None, None),
        P(("groups", "row", "rep")),
        P(("groups", "row", "rep")),
        P(("groups", "row", "rep")),
        P(),
        P(),
        P(("groups", "row", "rep"), None),
    )
    out_specs = (P(("groups", "row", "rep"), None), P("groups", None), P("groups", None))
    return jax.shard_map(shards, mesh=mesh, in_specs=in_specs, out_specs=out_specs, check_vma=False)
```

```python
import functools

import jax
import jax.numpy as jnp
from jax import lax
from jax.experimental import pallas as pl
from jax.experimental.pallas import tpu as pltpu
from jax.sharding import PartitionSpec as P

F32 = jnp.float32
BF16 = jnp.bfloat16
VMEM = pl.BlockSpec(memory_space=pltpu.VMEM)
SMEM = pl.BlockSpec(memory_space=pltpu.SMEM)
HBM = pl.BlockSpec(memory_space=pltpu.HBM)
MIB = 1 << 20
FIRST = ((7, 4), (6, 5), (1, 3), (0, 2))
SECOND = ((0, 2), (1, 3), (6, 4), (7, 5))
LATE = 3
PIECE = 16


def dot(a, b, ca=1, cb=0):
    return lax.dot_general(a, b, (((ca,), (cb,)), ((), ())), preferred_element_type=F32)


def half_of(block, blocks):
    bits = blocks.bit_length() - 1
    top = block >> (bits - 1)
    return (top ^ (block >> max(bits - 2, 0))) & 1 if bits > 1 else top


def masks_of(pair, blocks):
    steps = blocks // 2
    return [place + steps * (half_of(place, blocks) ^ core) for core, place in enumerate(pair)]


def places(blocks, masks):
    steps = blocks // 2
    if steps != len(masks):
        return [(k, k) for k in range(steps)]
    return [(a % steps, b % steps) for a, b in masks]


def densify_kernel(
    blocks, chunks, count_ref, row_hbm, col_hbm, adj_ref, keep_ref, send_ref, tiles, total, rows, cols, sems, small
):
    slots, edge = tiles.shape[0], tiles.shape[1]
    per = slots // chunks
    steps = blocks // 2
    side = jnp.bitwise_xor(half_of(lax.axis_index("row"), blocks), lax.axis_index("rep"))

    def copy(k):
        part = pl.ds(k * per, per)
        return pltpu.make_async_copy(adj_ref.at[part], tiles.at[part], sems.at[k])

    tables = [
        pltpu.make_async_copy(src, dst, small.at[i]) for i, (src, dst) in enumerate(((row_hbm, rows), (col_hbm, cols)))
    ]
    for table in tables:
        table.start()
    for k in range(chunks):
        copy(k).start()

    @pl.loop(0, 2 * blocks)
    def _(i):
        total[i] = jnp.zeros((edge, edge), F32)

    for table in tables:
        table.wait()
    count = count_ref[0]
    for k in range(chunks):
        copy(k).wait()

        @pl.loop(k * per, (k + 1) * per, unroll=4)
        def _(t):
            col = cols[t]
            away = jnp.bitwise_xor(half_of(col, blocks), side)
            where = (away * 2 + rows[t]) * steps + jnp.bitwise_and(col, steps - 1)
            where = jnp.where(t < count, where, 2 * blocks)
            total[where] += tiles[t].astype(F32)

    @pl.loop(0, steps, unroll=min(steps, 8))
    def _(i):
        at = pl.ds(pl.multiple_of(i * edge, edge), edge)
        for p in range(2):
            send_ref[p, :, at] = total[(2 + p) * steps + i].astype(BF16)
            keep_ref[p, :, at] = total[p * steps + i].astype(BF16)


def densify(tile_row, tile_col, tile_count, adjacency, blocks):
    slots, edge, _ = adjacency.shape
    chunks = 8
    half = jax.ShapeDtypeStruct((2, edge, blocks // 2 * edge), BF16)
    return pl.pallas_call(
        functools.partial(densify_kernel, blocks, chunks),
        out_shape=(half, half),
        in_specs=[SMEM, HBM, HBM, HBM],
        out_specs=(VMEM, VMEM),
        scratch_shapes=[
            pltpu.VMEM((slots, edge, edge), BF16),
            pltpu.VMEM((2 * blocks + 1, edge, edge), F32),
            pltpu.SMEM((slots,), jnp.int32),
            pltpu.SMEM((slots,), jnp.int32),
            pltpu.SemaphoreType.DMA((chunks,)),
            pltpu.SemaphoreType.DMA((2,)),
        ],
        compiler_params=pltpu.CompilerParams(vmem_limit_bytes=48 * MIB),
        cost_estimate=pl.CostEstimate(flops=10**9, bytes_accessed=12 * 10**6, transcendentals=0),
        name="densify",
    )(tile_count, *(pltpu.with_memory_space_constraint(x, pltpu.HBM) for x in (tile_row, tile_col, adjacency)))


def span(start, size):
    return pl.ds(pl.multiple_of(start * size, size), size)


def position(steps, pair):
    which = jnp.where(lax.axis_index("rep") == 0, pair[0], pair[1])
    return jnp.bitwise_xor(jnp.bitwise_and(lax.axis_index("row"), steps - 1), which)


def terms_kernel(order, keep_ref, recv_ref, cot_own_ref, cot_other_ref, x_own_ref, x_other_ref, *out_refs):
    nodes, _ = x_own_ref.shape
    classes = cot_own_ref.shape[0]
    rep = lax.axis_index("rep")
    away = 1 - rep
    cot_own, cot_other = cot_own_ref[...], cot_other_ref[...]
    for k, out in enumerate(out_refs):
        at = span(position(len(order), order[k]), nodes)
        out[span(rep, nodes), :] = x_own_ref[...]
        out[span(away, nodes), :] = x_other_ref[...]
        for base, a_ref in ((rep, keep_ref), (away, recv_ref)):
            term = dot(cot_own, a_ref[rep, :, at]) + dot(cot_other, a_ref[away, :, at])
            out[pl.ds(pl.multiple_of(2 * nodes + base * classes, 16), classes), :] = term.astype(BF16)


def aggregate_kernel(order, keep_ref, recv_ref, *refs):
    *x_refs, out_ref = refs
    nodes = keep_ref.shape[1]
    rep = lax.axis_index("rep")
    away = 1 - rep
    parts = [0.0, 0.0]
    back = 0.0
    for k, x_ref in enumerate(x_refs):
        at = span(position(len(order), order[k]), nodes)
        x_own, x_other = x_ref[span(rep, nodes), :], x_ref[span(away, nodes), :]
        for p in range(2):
            parts[p] += dot(keep_ref[p, :, at], x_own) + dot(recv_ref[p, :, at], x_other)
        back += x_ref[2 * nodes :, :].astype(F32)
    for p in range(2):
        out_ref[p * nodes : (p + 1) * nodes, :] = parts[p].astype(BF16)
    out_ref[2 * nodes :, :] = back.astype(BF16)


def total_kernel(a_ref, b_ref, o_ref):
    o_ref[...] = (a_ref[...].astype(F32) + b_ref[...].astype(F32)).astype(BF16)


def small_call(kernel, out, name, flops, *args, scratch=()):
    return pl.pallas_call(
        kernel,
        out_shape=out,
        scratch_shapes=scratch,
        in_specs=[VMEM] * len(args),
        out_specs=jax.tree.map(lambda _: VMEM, out),
        compiler_params=pltpu.CompilerParams(vmem_limit_bytes=44 * MIB),
        cost_estimate=pl.CostEstimate(flops=flops, bytes_accessed=10**6, transcendentals=0),
        name=name,
    )(*args)


def block_terms(place, x_ref, keep_ref, recv_ref, win_ref, wout_ref, own_ref, other_ref, proj):
    nodes = keep_ref.shape[1]
    classes = wout_ref.shape[0]
    rep = lax.axis_index("rep")
    away = 1 - rep
    agg = x_ref[: 2 * nodes, :]
    back = jnp.concatenate([x_ref[2 * nodes : 2 * nodes + classes, :], x_ref[2 * nodes + classes :, :]], axis=1)
    half = dot(agg, win_ref[...] * 0.5)
    tan = jnp.tanh(half)
    rise = 1.0 + tan
    hidden = (half * rise).astype(BF16)
    gate = rise * (1.0 + half * (1.0 - tan))
    grad_pre = (dot(back, wout_ref[...] * 0.5, 0, 0) * gate).astype(BF16)
    proj[...] = dot(wout_ref[...], hidden, 1, 1).astype(BF16)
    mine, theirs = proj[:, span(rep, nodes)], proj[:, span(away, nodes)]
    at = span(place, nodes)
    for ref, p in ((other_ref, away), (own_ref, rep)):
        ref[...] += dot(mine, keep_ref[p, :, at], 1, 1) + dot(theirs, recv_ref[p, :, at], 1, 1)
    return dot(agg, grad_pre, 0, 0), dot(back, hidden)


def early_kernel(places, keep_ref, recv_ref, win_ref, wout_ref, *refs):
    *x_refs, own_ref, other_ref, grads_ref, proj = refs
    steps = grads_ref.shape[0]
    width = win_ref.shape[0]
    own_ref[...] = jnp.zeros_like(own_ref)
    other_ref[...] = jnp.zeros_like(other_ref)
    for x_ref, pair in zip(x_refs, places):
        place = position(steps, pair)
        gin, gout = block_terms(place, x_ref, keep_ref, recv_ref, win_ref, wout_ref, own_ref, other_ref, proj)
        grads_ref[place, :width, :] = gin
        grads_ref[place, width:, :] = gout


def late_kernel(pair, keep_ref, recv_ref, win_ref, wout_ref, x_ref, own_in, other_in, grads_ref, *refs):
    own_ref, grad_ref, other_ref, last, proj = refs
    steps, rows, _ = grads_ref.shape
    width = win_ref.shape[0]
    nodes = own_ref.shape[1]
    own_ref[...] = own_in[...]
    other_ref[...] = other_in[...]
    place = position(steps, pair)
    gin, gout = block_terms(place, x_ref, keep_ref, recv_ref, win_ref, wout_ref, own_ref, other_ref, proj)
    last[:width, :] = gin
    last[width:, :] = gout
    total = jnp.where(place == 0, last[...], grads_ref[0])
    for i in range(1, steps):
        total += jnp.where(place == i, last[...], grads_ref[i])
    grad_ref[:rows, :] = total.astype(BF16)
    grad_ref[rows:, :] = jnp.zeros_like(grad_ref[rows:, :])
    for i in range(other_ref.shape[0] // PIECE):
        grad_ref[rows:, i * nodes : (i + 1) * nodes] = other_ref[i * PIECE : (i + 1) * PIECE, :].astype(BF16)


def finish_kernel(lo_ref, go_ref, gr_ref, logits_ref, gin_ref, gout_ref):
    width = gin_ref.shape[0]
    classes, nodes = logits_ref.shape
    rows = width + classes
    for i in range(classes // PIECE):
        at = slice(i * PIECE, (i + 1) * PIECE)
        logits_ref[at, :] = lo_ref[at, :] + gr_ref[rows:, i * nodes : (i + 1) * nodes].astype(F32)
    gin_ref[...] = go_ref[:width, :].astype(F32) + gr_ref[:width, :].astype(F32)
    gout_ref[...] = go_ref[width:rows, :].astype(F32) + gr_ref[width:rows, :].astype(F32)


def shards(features, adjacency, tile_row, tile_col, tile_count, weight_in, weight_out, cotangent):
    blocks = lax.axis_size("row")
    edge = adjacency.shape[1]
    width = features.shape[1]
    classes = weight_out.shape[1]

    steps = blocks // 2

    first, second = places(blocks, FIRST), places(blocks, SECOND)

    def partner(x, pair, masks=None):
        masks = masks or masks_of(pair, blocks)
        pairs = [(2 * r + p, 2 * (r ^ masks[p]) + p) for r in range(blocks) for p in range(2)]
        return lax.ppermute(x, ("row", "rep"), pairs)

    def swap(x):
        return lax.ppermute(x, "rep", [(0, 1), (1, 0)])

    wout = weight_out.T
    cot = cotangent.T
    hidden = weight_in.shape[1]
    rows = 2 * (edge + classes)

    def like(*shape, dtype=F32):
        return jax.ShapeDtypeStruct(shape, dtype)

    packed = like(rows, width, dtype=BF16)
    keep, send = densify(tile_row, tile_col, tile_count, adjacency, blocks)
    recv = swap(send)
    loads = small_call(
        functools.partial(terms_kernel, first), (packed,) * steps, "terms", 10**8, keep, recv, cot, swap(cot), features, swap(features)
    )
    arrived = [partner(load, pair) for load, pair in zip(loads, first)]
    part = small_call(functools.partial(aggregate_kernel, first), packed, "aggregate", 10**8, keep, recv, *arrived)
    load = small_call(total_kernel, packed, "total", 10**6, part, swap(part))
    if steps == len(SECOND):
        held = [partner(load, pair) for pair in second[:3]]
        held.append(partner(held[2], None, (1, 1)))
    else:
        held = [partner(load, pair) for pair in second]
    part = like(classes, edge)
    gin, gout = like(width, hidden), like(classes, hidden)
    late = LATE if steps == len(SECOND) else steps - 1
    early = [k for k in range(steps) if k != late]
    weights = (keep, recv, weight_in, wout)
    proj = pltpu.VMEM((classes, 2 * edge), BF16)
    sums = small_call(
        functools.partial(early_kernel, [second[k] for k in early]),
        (part, part, like(steps, width + classes, hidden)),
        "early",
        10**8,
        *weights,
        *(held[k] for k in early),
        scratch=[proj],
    )
    logit_own, grad = small_call(
        functools.partial(late_kernel, second[late]),
        (part, like(width + classes + PIECE, hidden, dtype=BF16)),
        "late",
        10**8,
        *weights,
        held[late],
        *sums,
        scratch=[pltpu.VMEM(part.shape, F32), pltpu.VMEM((width + classes, hidden), F32), proj],
    )
    logits, grad_in, grad_out = small_call(
        finish_kernel, (part, gin, gout), "finish", 10**6, logit_own, grad, swap(grad)
    )
    return (logits.T, grad_in, grad_out.T)


def solution(mesh):
    in_specs = (
        P(("groups", "row", "rep"), None),
        P(("groups", "row", "rep"), None, None),
        P(("groups", "row", "rep")),
        P(("groups", "row", "rep")),
        P(("groups", "row", "rep")),
        P(),
        P(),
        P(("groups", "row", "rep"), None),
    )
    out_specs = (P(("groups", "row", "rep"), None), P("groups", None), P("groups", None))
    return jax.shard_map(shards, mesh=mesh, in_specs=in_specs, out_specs=out_specs, check_vma=False)
```
